32 devices in a mesh: ctx: 8 (over z, x), exp: 4 (over y, core).
Axes of the slice: x: 2, y: 2, z: 4, core: 2. Of those that a mesh axis runs over, the one named last changes fastest.
Arguments:
- attn_query: bfloat16 [8192, 2048], P('ctx', 'exp'), may hold values from -112 to 112
- attn_key: bfloat16 [8192, 2048], P('ctx', 'exp'), may hold values from -40 to 40
- attn_value: bfloat16 [8192, 2048], P('ctx', 'exp'), may hold values from -40 to 40
- prefix_state: float32 [8, 16, 128, 128], P('ctx', 'exp'), may hold values from -40960 to 40960
- moe_in: bfloat16 [8192, 2048], P(('ctx', 'exp')), may hold values from -6 to 6
- grad_out: bfloat16 [8192, 2048], P(('ctx', 'exp')), may hold values from -6 to 6
- router_gates: bfloat16 [8192, 1], P(('ctx', 'exp')), may hold values from 0.099609375 to 1
- expert_ids: int32 [8192, 1], P(('ctx', 'exp')), may hold values from 0 to 3; in each aligned block of 256 rows (0 to 255, 256 to 511, ...) at most 96 rows name the same one
- w_gate_up: bfloat16 [4, 2048, 1024], P('exp'), may hold values from -0.125 to 0.125
- w_down: bfloat16 [4, 512, 2048], P('exp'), may hold values from -0.25 to 0.25
- w_out: bfloat16 [2048, 2048], P('exp'), may hold values from -0.125 to 0.125
Outputs:
- grad_query: bfloat16 [8192, 2048], P('ctx', 'exp')
- grad_key: bfloat16 [8192, 2048], P('ctx', 'exp')
- grad_value: bfloat16 [8192, 2048], P('ctx', 'exp')
- grad_resid: bfloat16 [8192, 2048], P(('ctx', 'exp'))
- grad_gates: bfloat16 [8192, 1], P(('ctx', 'exp'))
- grad_gate_up: float32 [4, 2048, 1024], P('exp', 'ctx')
- grad_down: float32 [4, 512, 2048], P('exp', 'ctx')
The draws below stay inside these ranges and needn't reach their ends.
Inputs may be any that keep to these rules, and one draw needn't show every extreme that they name: `expert_ids`: among the 256 rows of one device (aligned blocks of rows) no expert is named more than 96 times, a bound that some block reaches.
All inputs are finite; a program needn't handle non-finite values.
Results may differ from the reference program's by a relative error of at most 0.0063.
Values may be sent and summed in bfloat16 or wider, within the bound.
A program may use at most 192 MiB of HBM per device.

```python
import math
import jax
import jax.numpy as jnp
import numpy as np
from jax import lax

D = 2048
FF = 512
HEADS = 16
HEAD_DIM = 128
TOPK = 1
ROWS = 256
FLIGHT = 4
TOK_CTX = 1024
TOKENS = 8192
BLOCKS = 8
CAP = 96


def levels(stream_key, extent, split, least, high):
    def one(axis_at, parts):
        heights = jax.random.uniform(jax.random.fold_in(jax.random.fold_in(stream_key, 6), axis_at), (parts,), jnp.float32, least / len(split), high / len(split))
        return jnp.repeat(jnp.exp(heights), extent[axis_at] // parts).reshape((-1,) + (1,) * (len(extent) - axis_at - 1))

    level = one(*split[0])
    for cut in split[1:]:
        level = level * one(*cut)
    return level


def assign_block(own_key, own, number, rows, amount, top, reach, slope):
    order = jax.random.permutation(own_key, amount)
    heavy_load, common = shares(amount, rows * top, reach, slope, True), shares(amount, rows * top, reach, slope, False)
    places = jnp.arange(amount)

    def named(lengths, turn):
        used = int((lengths > 0).sum())
        fixed = max(1, used // 4)
        passed = fixed + (places - fixed + turn * (used - fixed)) % max(1, amount - fixed)
        return jnp.zeros((amount,), jnp.int32).at[order[jnp.where(places < fixed, places, passed)]].set(jnp.asarray(lengths, jnp.int32))

    lengths = jnp.where(number % 4 == 0, named(heavy_load, number // 4), named(common, number - number // 4 - 1))
    mixed = jax.random.permutation(jax.random.fold_in(own, 3), amount)
    donor, receiver = mixed[0:amount // 2 * 2:2], mixed[1:amount // 2 * 2:2]
    margin = jnp.minimum(lengths[donor] - 1, reach - lengths[receiver]) // 2
    margin = jnp.where((donor == order[0]) | (receiver == order[0]) | (lengths[receiver] == 0), 0, jnp.maximum(margin, 0))
    passed = jax.random.randint(jax.random.fold_in(own, 4), (amount // 2,), 0, 1 << 20) % (margin + 1)
    lengths = lengths.at[donor].add(-passed).at[receiver].add(passed)
    members = jnp.searchsorted(jnp.cumsum(lengths), jnp.arange(rows * top), side="right").astype(jnp.int32)
    table = members.reshape(top, rows).T
    table = table[jax.random.permutation(jax.random.fold_in(own, 1), rows)]
    turn = jax.random.randint(jax.random.fold_in(own, 2), (rows, 1), 0, top)
    return jnp.take_along_axis(table, (jnp.arange(top)[None, :] + turn) % top, axis=1)


def shares(number_of, total, most, skew, full):
    loads = [(1 << 20) // math.isqrt(rank ** skew) + 1 for rank in range(1, number_of + 1)]
    largest = most if full else min(most, max(-(-total // number_of), total * loads[0] // sum(loads)))
    least = 1 if total - largest >= number_of - 1 else 0
    holding, rest = [largest] + [least] * (number_of - 1), total - largest - least * (number_of - 1)
    while rest > 0:
        movable = [i for i in range(1, number_of) if holding[i] < largest] or [i for i in range(1, number_of) if holding[i] < most]
        pool, remaining = sum([loads[i] for i in movable]), rest
        for i in movable:
            more = min(most - holding[i], max(1, remaining * loads[i] // pool), rest)
            holding[i] = holding[i] + more
            rest = rest - more
    return np.array(holding)


def scatter_about(key, shape, scale, bound, split=(), kind=jnp.bfloat16):
    values = scale * jax.random.normal(key, shape, jnp.float32)
    if split:
        values = values * levels(key, shape, split, -0.22, 0.18)
    return jnp.clip(values, -bound, bound).astype(kind)


def setup_inputs(seed: int = 0) -> dict:
    seeds = jax.random.split(jax.random.key(seed), 12)
    attn_query = scatter_about(seeds[0], (TOKENS, HEADS * HEAD_DIM), (0.1 * (4 * TOKENS) ** 0.5), 112.0, ((0, 8), (1, 4)))
    attn_key = scatter_about(seeds[1], (TOKENS, HEADS * HEAD_DIM), (0.5 * (4 * TOKENS) ** 0.25), 40.0, ((0, 8), (1, 4)))
    attn_value = scatter_about(seeds[2], (TOKENS, HEADS * HEAD_DIM), (0.5 * (4 * TOKENS) ** 0.25), 40.0, ((0, 8), (1, 4)))
    prefix_state = scatter_about(seeds[3], (BLOCKS, HEADS, HEAD_DIM, HEAD_DIM), (0.25 * (3 * TOKENS) ** 0.5 * (4 * TOKENS) ** 0.5), 40960.0, ((0, 8), (1, 4)), jnp.float32)
    moe_in = scatter_about(seeds[4], (TOKENS, D), 1.0, 6.0, ((0, 32),))
    grad_out = scatter_about(seeds[5], (TOKENS, D), 0.5, 6.0, ((0, 32),))
    router_gates = jnp.clip(0.099609375 + 0.9003906 * jax.random.uniform(seeds[6], (TOKENS, TOPK), jnp.float32) ** levels(seeds[6], (TOKENS, TOPK), ((0, 32),), -0.2, 0.2), 0.099609375, 1.0).astype(jnp.bfloat16)
    expert_ids_keys = jax.random.split(jax.random.fold_in(seeds[7], 1), TOKENS // ROWS)
    expert_ids_turns = jax.random.permutation(jax.random.fold_in(seeds[7], 3), TOKENS // ROWS)
    expert_ids = jax.vmap(lambda own, number: assign_block(jax.random.fold_in(seeds[7], 2), own, number, ROWS, FLIGHT, TOPK, CAP, 1))(expert_ids_keys, expert_ids_turns).reshape((TOKENS, TOPK))
    w_gate_up = scatter_about(seeds[8], (FLIGHT, D, 2 * FF), D ** -0.5, 0.125, ((0, 4),))
    w_down = scatter_about(seeds[9], (FLIGHT, FF, D), FF ** -0.5, 0.25, ((0, 4),))
    w_out = scatter_about(seeds[10], (HEADS * HEAD_DIM, D), (HEADS * HEAD_DIM) ** -0.5, 0.125, ((0, 4),))
    return dict(attn_query=attn_query, attn_key=attn_key, attn_value=attn_value, prefix_state=prefix_state, moe_in=moe_in, grad_out=grad_out, router_gates=router_gates, expert_ids=expert_ids, w_gate_up=w_gate_up, w_down=w_down, w_out=w_out)


highest = lax.Precision.HIGHEST


def silu_slope(value):
    logistic = jax.nn.sigmoid(value)
    return logistic * (1.0 + value * (1.0 - logistic))


def contract_rows(left, right):
    return lax.dot_general(left, right, (((0,), (0,)), ((), ())), preferred_element_type=jnp.float32)


def contract_cols(left, right):
    return lax.dot_general(left, right, (((1,), (1,)), ((), ())), preferred_element_type=jnp.float32)


def expert_backward(inputs, gate_vals, w_pair, w_back, hidden_units):
    width = w_back.shape[1]
    rows_in = inputs[:, :width]
    cotangent = inputs[:, width:]
    both = jnp.dot(rows_in, w_pair, preferred_element_type=jnp.float32)
    first = both[:, :hidden_units]
    second = both[:, hidden_units:]
    hidden = (jax.nn.silu(first) * second).astype(jnp.bfloat16)
    output = jnp.dot(hidden, w_back, preferred_element_type=jnp.float32)
    cot_wide = cotangent.astype(jnp.float32)
    grad_gate = jnp.sum(cot_wide * output, axis=1).astype(jnp.bfloat16)
    scaled = (gate_vals.astype(jnp.float32)[:, None] * cot_wide).astype(jnp.bfloat16)
    grad_hidden = contract_cols(scaled, w_back)
    grad_first = grad_hidden * second * silu_slope(first)
    grad_second = grad_hidden * jax.nn.silu(first)
    grad_both = jnp.concatenate([grad_first, grad_second], axis=1).astype(jnp.bfloat16)
    grad_rows = contract_cols(grad_both, w_pair).astype(jnp.bfloat16)
    return rows_in, hidden, scaled, grad_both, grad_rows, grad_gate


def block_state(query_rows, grad_rows, counts):
    query_wide = query_rows.astype(jnp.float32)
    grad_wide = grad_rows.astype(jnp.float32) / counts[:, None, None]
    return jnp.einsum("uhj,uhi->hji", query_wide, grad_wide, precision=highest)


def attend_block(query_rows, key_rows, value_rows, grad_rows, prior, later, counts):
    scale_col = counts[:, None, None]
    inverse = 1.0 / counts
    position = jnp.arange(counts.shape[0], dtype=jnp.int32)
    lower = (position[None, :] <= position[:, None]).astype(jnp.float32)
    upper = (position[None, :] >= position[:, None]).astype(jnp.float32) * inverse[None, :]
    mix_query = (jnp.einsum("thd,uhd->htu", grad_rows, value_rows, preferred_element_type=jnp.float32)
                 * lower).astype(jnp.bfloat16)
    grad_query = (jnp.einsum("htu,uhd->thd", mix_query, key_rows, preferred_element_type=jnp.float32)
                  + jnp.einsum("thi,hji->thj", grad_rows.astype(jnp.float32), prior, precision=highest)) / scale_col
    mix_key = (jnp.einsum("thd,uhd->htu", value_rows, grad_rows, preferred_element_type=jnp.float32)
               * upper).astype(jnp.bfloat16)
    grad_key = (jnp.einsum("htu,uhd->thd", mix_key, query_rows, preferred_element_type=jnp.float32)
                + jnp.einsum("thi,hji->thj", value_rows.astype(jnp.float32), later, precision=highest))
    mix_value = (jnp.einsum("thd,uhd->htu", key_rows, query_rows, preferred_element_type=jnp.float32)
                 * upper).astype(jnp.bfloat16)
    grad_value = (jnp.einsum("htu,uhd->thd", mix_value, grad_rows, preferred_element_type=jnp.float32)
                  + jnp.einsum("thj,hji->thi", key_rows.astype(jnp.float32), later, precision=highest))
    return grad_query, grad_key, grad_value


def reference(attn_query, attn_key, attn_value, prefix_state, moe_in, grad_out, router_gates, expert_ids, w_gate_up, w_down, w_out):
    pair_total = TOKENS * TOPK
    block_count = TOKENS // ROWS
    flat_ids = expert_ids.reshape(pair_total)
    member = (flat_ids[:, None] == jnp.arange(FLIGHT, dtype=jnp.int32)[None, :]).astype(jnp.int32)
    member = member.reshape(block_count, ROWS * TOPK, FLIGHT)
    earlier = jnp.cumsum(member, axis=1) - member
    slot_of = jnp.sum(earlier * member, axis=2).reshape(pair_total)
    block_of = jnp.arange(pair_total, dtype=jnp.int32) // (ROWS * TOPK)
    table = jnp.full((FLIGHT, block_count * CAP), pair_total, jnp.int32)
    table = table.at[flat_ids, block_of * CAP + slot_of].set(jnp.arange(pair_total, dtype=jnp.int32))
    flat_gates = router_gates.reshape(pair_total)

    def one_expert(inputs):
        listing, w_pair, w_back = inputs
        token_of = listing // TOPK
        rows_in = jnp.take(moe_in, token_of, axis=0, mode="fill", fill_value=0)
        cotangent = jnp.take(grad_out, token_of, axis=0, mode="fill", fill_value=0)
        gate_vals = jnp.take(flat_gates, listing, axis=0, mode="fill", fill_value=0)
        joined = jnp.concatenate([rows_in, cotangent], axis=1)
        rows_in, hidden, scaled, grad_both, grad_rows, grad_gate = expert_backward(joined, gate_vals, w_pair, w_back, FF)
        return grad_rows, grad_gate, contract_rows(rows_in, grad_both), contract_rows(hidden, scaled)

    grad_rows, grad_gate, grad_gate_up, grad_down = lax.map(one_expert, (table, w_gate_up, w_down))
    flat_table = table.reshape(-1)
    pair_rows = jnp.zeros((pair_total, D), jnp.float32).at[flat_table].set(
        grad_rows.reshape(-1, D).astype(jnp.float32), mode="drop")
    grad_resid = (grad_out.astype(jnp.float32) + pair_rows.reshape(TOKENS, TOPK, D).sum(axis=1)).astype(jnp.bfloat16)
    grad_gates = jnp.zeros((pair_total,), jnp.bfloat16).at[flat_table].set(
        grad_gate.reshape(-1), mode="drop").reshape(TOKENS, TOPK)
    attn_grad = contract_cols(grad_resid, w_out).astype(jnp.bfloat16)

    block_shape = (BLOCKS, TOK_CTX, HEADS, HEAD_DIM)
    block_ids = jnp.arange(BLOCKS, dtype=jnp.int32)

    def counts_of(block):
        return (3 * TOKENS + block * TOK_CTX + jnp.arange(TOK_CTX, dtype=jnp.int32) + 1).astype(jnp.float32)

    def state_of(inputs):
        query, grad, block = inputs
        return block_state(query, grad, counts_of(block))

    queries = attn_query.reshape(block_shape)
    keys_all = attn_key.reshape(block_shape)
    values_all = attn_value.reshape(block_shape)
    grads_all = attn_grad.reshape(block_shape)
    states = lax.map(state_of, (queries, grads_all, block_ids))
    totals = jnp.cumsum(states[::-1], axis=0)[::-1]
    later_all = jnp.concatenate([totals[1:], jnp.zeros_like(states[:1])], axis=0)

    def grads_of(inputs):
        query, key_rows, value_rows, grad, prior, later, block = inputs
        results = attend_block(query, key_rows, value_rows, grad, prior, later, counts_of(block))
        return tuple(result.reshape(TOK_CTX, HEADS * HEAD_DIM).astype(jnp.bfloat16) for result in results)

    grad_query, grad_key, grad_value = lax.map(
        grads_of, (queries, keys_all, values_all, grads_all, prefix_state, later_all, block_ids))
    flat_shape = (TOKENS, HEADS * HEAD_DIM)
    return (grad_query.reshape(flat_shape), grad_key.reshape(flat_shape), grad_value.reshape(flat_shape),
            grad_resid, grad_gates, grad_gate_up, grad_down)
```

```python
import functools

import jax
import jax.numpy as jnp
from jax import lax
from jax.experimental import pallas as pl
from jax.experimental.pallas import tpu as pltpu
from jax.sharding import PartitionSpec as P

LANES = 128


def contract_rows(left, right):
    return lax.dot_general(
        left, right, (((0,), (0,)), ((), ())), preferred_element_type=jnp.float32
    )


def contract_cols(left, right):
    return lax.dot_general(
        left, right, (((1,), (1,)), ((), ())), preferred_element_type=jnp.float32
    )


def plain(left, right):
    return jnp.dot(left, right, preferred_element_type=jnp.float32)


def flip(value, axis, bit, size):
    return lax.ppermute(value, axis, [(i, i ^ bit) for i in range(size)])


def expert_backward(inputs, width, w_pair, w_back):
    hidden_units = w_back.shape[0]
    rows_in = inputs[:, :width]
    cotangent = inputs[:, width : 2 * width]
    gate_vals = inputs[:, 2 * width : 2 * width + 1].astype(jnp.float32)
    both = plain(rows_in, w_pair)
    first = both[:, :hidden_units]
    second = both[:, hidden_units:]
    logistic = jax.nn.sigmoid(first)
    silu = first * logistic
    hidden = (silu * second).astype(jnp.bfloat16)
    output = plain(hidden, w_back)
    cot_wide = cotangent.astype(jnp.float32)
    grad_gate = jnp.sum(cot_wide * output, axis=1, keepdims=True).astype(jnp.bfloat16)
    scaled = (gate_vals * cot_wide).astype(jnp.bfloat16)
    grad_hidden = contract_cols(scaled, w_back)
    slope = logistic * (1.0 + first * (1.0 - logistic))
    grad_both = jnp.concatenate(
        [grad_hidden * second * slope, grad_hidden * silu], axis=1
    ).astype(jnp.bfloat16)
    grad_rows = contract_cols(grad_both, w_pair).astype(jnp.bfloat16)
    return rows_in, hidden, scaled, grad_both, grad_rows, grad_gate


def scatter_sum(left, right, axis, bits):
    size = lax.axis_size(axis)
    levels = size.bit_length() - 1
    me = lax.axis_index(axis)
    tokens, rows = left.shape
    cols = right.shape[1]
    shape = [2] * levels
    pos = {bit: levels - 1 - bit for bit in range(levels)}
    split = left.reshape([tokens] + shape + [rows // size])
    first = bits[0]
    mine = (me >> first) & 1

    def part(which):
        chosen = lax.dynamic_index_in_dim(split, which, axis=1 + pos[first], keepdims=False)
        return contract_rows(chosen.reshape(tokens, rows // 2), right)

    away = flip(part(1 - mine).astype(jnp.bfloat16), axis, 1 << first, size)
    total = part(mine) + away.astype(jnp.float32)
    left_bits = [bit for bit in range(levels) if bit != first]
    for bit in bits[1:]:
        order = sorted(left_bits, reverse=True)
        spread = total.reshape([2] * len(order) + [rows // size, cols])
        mine = (me >> bit) & 1
        dim = order.index(bit)
        send = lax.dynamic_index_in_dim(spread, 1 - mine, axis=dim, keepdims=False)
        keep = lax.dynamic_index_in_dim(spread, mine, axis=dim, keepdims=False)
        away = flip(send.astype(jnp.bfloat16), axis, 1 << bit, size)
        total = keep + away.astype(jnp.float32)
        left_bits.remove(bit)
    return total.reshape(1, rows // size, cols)


def state_kernel(query_ref, grad_ref, inv_ref, state_ref, scaled_ref):
    scaled = (grad_ref[...].astype(jnp.float32) * inv_ref[...]).astype(jnp.bfloat16)
    scaled_ref[...] = scaled
    state_ref[0] = contract_rows(query_ref[...], scaled)


def forward_kernel(chunk, key_ref, value_ref, grad_ref, inv_ref, prior_ref, out_ref):
    tokens = key_ref.shape[0]
    row = lax.broadcasted_iota(jnp.int32, (chunk, chunk), 0)
    col = lax.broadcasted_iota(jnp.int32, (chunk, chunk), 1)
    state = prior_ref[0]
    for at in range(tokens // chunk):
        rows = pl.ds(at * chunk, chunk)
        keys, values, grads = key_ref[rows, :], value_ref[rows, :], grad_ref[rows, :]
        mix = jnp.where(col <= row, contract_cols(grads, values), 0.0).astype(jnp.bfloat16)
        out = plain(mix, keys) + contract_cols(grads, state.astype(jnp.bfloat16))
        out_ref[rows, :] = (out * inv_ref[rows, :]).astype(jnp.bfloat16)
        state = state + contract_rows(keys, values)


def backward_kernel(chunk, query_ref, key_ref, value_ref, scaled_ref, later_ref, dkey_ref, dvalue_ref):
    tokens = key_ref.shape[0]
    row = lax.broadcasted_iota(jnp.int32, (chunk, chunk), 0)
    col = lax.broadcasted_iota(jnp.int32, (chunk, chunk), 1)
    state = later_ref[0]
    for at in reversed(range(tokens // chunk)):
        rows = pl.ds(at * chunk, chunk)
        query, keys, values, scaled = query_ref[rows, :], key_ref[rows, :], value_ref[rows, :], scaled_ref[rows, :]
        held = state.astype(jnp.bfloat16)
        mix_key = jnp.where(col >= row, contract_cols(values, scaled), 0.0).astype(jnp.bfloat16)
        dkey_ref[rows, :] = (plain(mix_key, query) + contract_cols(values, held)).astype(jnp.bfloat16)
        mix_value = jnp.where(col >= row, contract_cols(keys, query), 0.0).astype(jnp.bfloat16)
        dvalue_ref[rows, :] = (plain(mix_value, scaled) + plain(keys, held)).astype(jnp.bfloat16)
        state = state + contract_rows(query, scaled)


def on_device(
    attn_query,
    attn_key,
    attn_value,
    prefix_state,
    moe_in,
    grad_out,
    router_gates,
    expert_ids,
    w_gate_up,
    w_down,
    w_out,
):
    groups = lax.axis_size("exp")
    blocks_total = lax.axis_size("ctx")
    flight = w_gate_up.shape[0] * groups
    rows, width = moe_in.shape
    capacity = 3 * rows // (2 * flight)
    flat_ids = expert_ids.reshape(rows)
    place = jnp.arange(rows, dtype=jnp.int32)
    same = (flat_ids[:, None] == flat_ids[None, :]) & (place[:, None] < place[None, :])
    slot_of = jnp.sum(same.astype(jnp.int32), axis=0)
    target = flat_ids * capacity + slot_of
    placing = (jnp.arange(flight * capacity, dtype=jnp.int32)[:, None] == target[None, :]).astype(
        jnp.bfloat16
    )
    joined = jnp.concatenate(
        [moe_in, grad_out, jnp.broadcast_to(router_gates, (rows, LANES))], axis=1
    )
    packed = plain(placing, joined).astype(jnp.bfloat16)
    inputs = lax.all_to_all(packed, "exp", split_axis=0, concat_axis=0, tiled=True)
    rows_in, hidden, scaled, grad_both, grad_rows, grad_gate = expert_backward(
        inputs, width, w_gate_up[0], w_down[0]
    )
    rows_back = jnp.concatenate(
        [grad_rows, jnp.broadcast_to(grad_gate, (grad_rows.shape[0], LANES))], axis=1
    )
    returned = lax.all_to_all(rows_back, "exp", split_axis=0, concat_axis=0, tiled=True)
    pair_grads = contract_rows(placing, returned)
    grad_resid = (grad_out.astype(jnp.float32) + pair_grads[:, :width]).astype(jnp.bfloat16)
    grad_gates = pair_grads[:, width : width + 1].astype(jnp.bfloat16)

    levels = blocks_total.bit_length() - 1
    rising = list(range(levels))
    turned = rising[1:] + rising[:1]
    grad_gate_up = scatter_sum(rows_in, grad_both, "ctx", rising)
    grad_down = scatter_sum(hidden, scaled, "ctx", turned)

    mine = lax.axis_index("exp")
    pieces = {0: grad_resid}
    heads_width = w_out.shape[0]
    attn_grad = jnp.zeros((rows * groups, heads_width), jnp.bfloat16)
    for k in range(1, groups):
        low = k & -k
        pieces[k] = flip(pieces[k - low], "exp", low, groups)
    for k in range(groups):
        piece = contract_cols(pieces[k], w_out).astype(jnp.bfloat16)
        attn_grad = lax.dynamic_update_slice(attn_grad, piece, ((mine ^ k) * rows, 0))

    head_dim = prefix_state.shape[-1]
    tokens = attn_query.shape[0]
    heads = attn_query.shape[1] // head_dim
    block_at = lax.axis_index("ctx")
    counts = (
        3 * tokens * blocks_total + block_at * tokens + jnp.arange(tokens, dtype=jnp.int32) + 1
    ).astype(jnp.float32)
    inverse = jnp.broadcast_to((1.0 / counts)[:, None], (tokens, head_dim))

    per_head = pl.BlockSpec((tokens, head_dim), lambda h: (0, h))
    fixed = pl.BlockSpec((tokens, head_dim), lambda h: (0, 0))
    one_state = pl.BlockSpec((1, head_dim, head_dim), lambda h: (h, 0, 0))
    flat = jax.ShapeDtypeStruct((tokens, heads * head_dim), jnp.bfloat16)
    states = jax.ShapeDtypeStruct((heads, head_dim, head_dim), jnp.float32)
    chunk = min(256, tokens)

    def cost(flops, moved):
        return pl.CostEstimate(flops=flops, bytes_accessed=moved, transcendentals=0)

    size = 2 * tokens * heads * head_dim
    local_state, grad_scaled = pl.pallas_call(
        state_kernel,
        grid=(heads,),
        in_specs=[per_head, per_head, fixed],
        out_specs=[one_state, per_head],
        out_shape=[states, flat],
        cost_estimate=cost(size * head_dim, 3 * size),
        name="state",
    )(attn_query, attn_grad, inverse)

    later = jnp.zeros_like(local_state)
    step = 1
    while step < blocks_total:
        held = (local_state + later).astype(jnp.bfloat16)
        came = lax.ppermute(held, "ctx", [(i, i - step) for i in range(step, blocks_total)])
        later = later + came.astype(jnp.float32)
        step *= 2

    grad_query = pl.pallas_call(
        functools.partial(forward_kernel, chunk),
        grid=(heads,),
        in_specs=[per_head, per_head, per_head, fixed, one_state],
        out_specs=per_head,
        out_shape=flat,
        cost_estimate=cost(size * (2 * chunk + 2 * head_dim), 4 * size),
        name="forward",
    )(attn_key, attn_value, attn_grad, inverse, prefix_state[0])
    grad_key, grad_value = pl.pallas_call(
        functools.partial(backward_kernel, chunk),
        grid=(heads,),
        in_specs=[per_head, per_head, per_head, per_head, one_state],
        out_specs=[per_head, per_head],
        out_shape=[flat, flat],
        cost_estimate=cost(size * (4 * chunk + 3 * head_dim), 6 * size),
        name="backward",
    )(attn_query, attn_key, attn_value, grad_scaled, later)
    return grad_query, grad_key, grad_value, grad_resid, grad_gates, grad_gate_up, grad_down


def solution(mesh):
    return jax.shard_map(
        on_device,
        mesh=mesh,
        in_specs=(
            P("ctx", "exp"),
            P("ctx", "exp"),
            P("ctx", "exp"),
            P("ctx", "exp", None, None),
            P(("ctx", "exp"), None),
            P(("ctx", "exp"), None),
            P(("ctx", "exp"), None),
            P(("ctx", "exp"), None),
            P("exp", None, None),
            P("exp", None, None),
            P("exp", None),
        ),
        out_specs=(
            P("ctx", "exp"),
            P("ctx", "exp"),
            P("ctx", "exp"),
            P(("ctx", "exp"), None),
            P(("ctx", "exp"), None),
            P("exp", "ctx", None),
            P("exp", "ctx", None),
        ),
        check_vma=False,
    )
```

```python
import functools

import jax
import jax.numpy as jnp
from jax import lax
from jax.experimental import pallas as pl
from jax.experimental.pallas import tpu as pltpu
from jax.sharding import PartitionSpec as P

LANES = 128


def contract_rows(left, right):
    return lax.dot_general(
        left, right, (((0,), (0,)), ((), ())), preferred_element_type=jnp.float32
    )


def contract_cols(left, right):
    return lax.dot_general(
        left, right, (((1,), (1,)), ((), ())), preferred_element_type=jnp.float32
    )


def plain(left, right):
    return jnp.dot(left, right, preferred_element_type=jnp.float32)


def flip(value, axis, bit, size):
    return lax.ppermute(value, axis, [(i, i ^ bit) for i in range(size)])


def expert_kernel(near, width, *refs):
    blocks, (pair_ref, back_ref) = refs[:near], refs[near : near + 2]
    rows_ref, hidden_ref, scaled_ref, both_ref = refs[near + 2 : near + 6]
    outs = refs[near + 6 :]
    capacity = blocks[0].shape[0]
    hidden_units = back_ref.shape[0]
    for at, block in enumerate(blocks):
        rows_ref[pl.ds(at * capacity, capacity), :] = block[:, :width]
    cot_wide = jnp.concatenate([block[:, width : 2 * width] for block in blocks], axis=0).astype(
        jnp.float32
    )
    gate_vals = jnp.concatenate([block[:, 2 * width :] for block in blocks], axis=0)
    scaled = (gate_vals[:, :1].astype(jnp.float32) * cot_wide).astype(jnp.bfloat16)
    scaled_ref[...] = scaled
    both = plain(rows_ref[...], pair_ref[...])
    first = both[:, :hidden_units]
    second = both[:, hidden_units:]
    logistic = jax.nn.sigmoid(first)
    silu = first * logistic
    hidden = (silu * second).astype(jnp.bfloat16)
    hidden_ref[...] = hidden
    grad_hidden = contract_cols(scaled, back_ref[...])
    slope = logistic * (1.0 + first * (1.0 - logistic))
    both_ref[:, :hidden_units] = (grad_hidden * second * slope).astype(jnp.bfloat16)
    both_ref[:, hidden_units:] = (grad_hidden * silu).astype(jnp.bfloat16)
    output = plain(hidden, back_ref[...])
    grad_gate = jnp.sum(cot_wide * output, axis=1, keepdims=True)
    grad_rows = contract_cols(both_ref[...], pair_ref[...]).astype(jnp.bfloat16)
    for at, out in enumerate(outs):
        rows = slice(at * capacity, (at + 1) * capacity)
        out[:, :width] = grad_rows[rows]
        out[:, width:] = jnp.broadcast_to(grad_gate[rows], (capacity, LANES)).astype(jnp.bfloat16)


def expert_backward(blocks, width, w_pair, w_back):
    near = len(blocks)
    capacity = blocks[0].shape[0]
    tokens = near * capacity
    hidden_units = w_back.shape[0]

    def shape(*dims):
        return jax.ShapeDtypeStruct(dims, jnp.bfloat16)

    outs = [shape(tokens, width), shape(tokens, hidden_units), shape(tokens, width)]
    outs += [shape(tokens, 2 * hidden_units)] + [shape(capacity, width + LANES)] * near
    whole = pl.BlockSpec(memory_space=pltpu.VMEM)
    return pl.pallas_call(
        functools.partial(expert_kernel, near, width),
        in_specs=[whole] * (near + 2),
        out_specs=[whole] * len(outs),
        out_shape=outs,
        cost_estimate=cost(12 * tokens * width * hidden_units, 24 * hidden_units * width),
        name="expert",
    )(*blocks, w_pair, w_back)


def after(value, *others):
    return lax.optimization_barrier((value,) + others)[0]


def cost(flops, moved):
    return pl.CostEstimate(flops=flops, bytes_accessed=moved, transcendentals=0)


def partial_kernel(by_rows, parts, me_ref, *refs):
    lefts, rights, came, out_ref = refs[:parts], refs[parts : 2 * parts], refs[2 * parts : -1], refs[-1]
    multiply = plain if by_rows else contract_rows
    total = multiply(lefts[0][...], rights[0][...])
    for left_ref, right_ref in zip(lefts[1:], rights[1:]):
        total = total + multiply(left_ref[...], right_ref[...])
    for one in came:
        total = total + one[0].astype(jnp.float32)
    out_ref[0] = total.astype(out_ref.dtype)


class ScatterSum:
    def __init__(self, lefts, rights, at, cols, axis, bits, by_rows, rows):
        self.lefts, self.rights, self.at, self.cols = lefts, rights, at, cols
        self.axis, self.bits, self.by_rows = axis, bits, by_rows
        self.size = lax.axis_size(axis)
        self.unit = rows // self.size
        self.me = lax.axis_index(axis).astype(jnp.int32).reshape(1)
        self.came = []

    def step(self, *ties):
        bits, stage, unit, cols, at = self.bits, len(self.came), self.unit, self.cols, self.at
        last = stage == len(bits)
        free = sorted(set(bits) - set(bits[: stage + 1]))

        def chunk(j, me_ref):
            own = me_ref[0]
            found = 0
            for bit in bits[: stage + 1]:
                found = found | (own & (1 << bit))
            if not last:
                found = found ^ (1 << bits[stage])
            for place, bit in enumerate(free):
                found = found | (((j >> place) & 1) << bit)
            return found

        def spot(upto):
            kept = sorted(set(bits) - set(bits[:upto]))

            def index(j, me_ref):
                found = chunk(j, me_ref)
                where = 0 * j
                for place, bit in enumerate(kept):
                    where = where | (((found >> bit) & 1) << place)
                return (where, 0, 0)

            return index

        steps = 1 << len(free)
        depth = self.rights[0].shape[0]
        if self.by_rows:
            left_spec = pl.BlockSpec((unit, depth), lambda j, me_ref: (chunk(j, me_ref), 0))
        else:
            left_spec = pl.BlockSpec((depth, unit), lambda j, me_ref: (0, chunk(j, me_ref)))
        right_spec = pl.BlockSpec((depth, cols), lambda j, me_ref: (0, at))
        parts = len(self.lefts)
        came = self.came
        if ties and came:
            came = came[:-1] + [after(came[-1], *ties)]
        kind = jnp.float32 if last else jnp.bfloat16
        out = pl.pallas_call(
            functools.partial(partial_kernel, self.by_rows, parts),
            grid_spec=pltpu.PrefetchScalarGridSpec(
                num_scalar_prefetch=1,
                grid=(steps,),
                in_specs=[left_spec] * parts
                + [right_spec] * parts
                + [pl.BlockSpec((1, unit, cols), spot(i + 1)) for i in range(stage)],
                out_specs=pl.BlockSpec((1, unit, cols), lambda j, me_ref: (j, 0, 0)),
            ),
            out_shape=jax.ShapeDtypeStruct((steps, unit, cols), kind),
            cost_estimate=cost(2 * parts * depth * unit * cols * steps, 4 * steps * unit * cols + 2 * depth * cols),
        )(self.me, *self.lefts, *self.rights, *came)
        if last:
            return out
        self.came = came + [flip(out, self.axis, 1 << bits[stage], self.size)]
        return None


def state_kernel(query_ref, grad_ref, inv_ref, state_ref, scaled_ref):
    scaled = (grad_ref[...].astype(jnp.float32) * inv_ref[...]).astype(jnp.bfloat16)
    scaled_ref[...] = scaled
    state_ref[0] = contract_rows(query_ref[...], scaled)


def forward_kernel(chunk, key_ref, value_ref, grad_ref, inv_ref, prior_ref, out_ref):
    tokens = key_ref.shape[0]
    row = lax.broadcasted_iota(jnp.int32, (chunk, chunk), 0)
    col = lax.broadcasted_iota(jnp.int32, (chunk, chunk), 1)
    state = prior_ref[0]
    for at in range(tokens // chunk):
        rows = pl.ds(at * chunk, chunk)
        keys, values, grads = key_ref[rows, :], value_ref[rows, :], grad_ref[rows, :]
        mix = jnp.where(col <= row, contract_cols(grads, values), 0.0).astype(jnp.bfloat16)
        out = plain(mix, keys) + contract_cols(grads, state.astype(jnp.bfloat16))
        out_ref[rows, :] = (out * inv_ref[rows, :]).astype(jnp.bfloat16)
        state = state + contract_rows(keys, values)


def backward_kernel(chunk, query_ref, key_ref, value_ref, scaled_ref, later_ref, dkey_ref, dvalue_ref):
    tokens = key_ref.shape[0]
    row = lax.broadcasted_iota(jnp.int32, (chunk, chunk), 0)
    col = lax.broadcasted_iota(jnp.int32, (chunk, chunk), 1)
    state = later_ref[0]
    for at in reversed(range(tokens // chunk)):
        rows = pl.ds(at * chunk, chunk)
        query, keys, values, scaled = query_ref[rows, :], key_ref[rows, :], value_ref[rows, :], scaled_ref[rows, :]
        held = state.astype(jnp.bfloat16)
        mix_key = jnp.where(col >= row, contract_cols(values, scaled), 0.0).astype(jnp.bfloat16)
        dkey_ref[rows, :] = (plain(mix_key, query) + contract_cols(values, held)).astype(jnp.bfloat16)
        mix_value = jnp.where(col >= row, contract_cols(keys, query), 0.0).astype(jnp.bfloat16)
        dvalue_ref[rows, :] = (plain(mix_value, scaled) + plain(keys, held)).astype(jnp.bfloat16)
        state = state + contract_rows(query, scaled)


def compute(
    attn_query,
    attn_key,
    attn_value,
    prefix_state,
    moe_in,
    grad_out,
    router_gates,
    expert_ids,
    w_gate_up,
    w_down,
    w_out,
):
    groups = lax.axis_size("exp")
    blocks_total = lax.axis_size("ctx")
    flight = w_gate_up.shape[0] * groups
    rows, width = moe_in.shape
    capacity = 3 * rows // (2 * flight)
    flat_ids = expert_ids.reshape(rows)
    place = jnp.arange(rows, dtype=jnp.int32)
    same = (flat_ids[:, None] == flat_ids[None, :]) & (place[:, None] < place[None, :])
    slot_of = jnp.sum(same.astype(jnp.int32), axis=0)
    mine = lax.axis_index("exp")
    target = (flat_ids ^ mine) * capacity + slot_of
    joined = jnp.concatenate(
        [moe_in, grad_out, jnp.broadcast_to(router_gates, (rows, LANES))], axis=1
    )
    place = jnp.arange(capacity, dtype=jnp.int32)[:, None]
    placing = {
        k: (place + k * capacity == target[None, :]).astype(jnp.bfloat16) for k in range(groups)
    }
    arrived = {}
    for k in reversed(range(groups)):
        packed = plain(placing[k], joined).astype(jnp.bfloat16)
        arrived[k] = flip(packed, "exp", k, groups) if k else packed
    near = groups // 2
    parts, returned = [], {}
    for low in (0, near):
        chosen = range(low, low + near)
        found = expert_backward([arrived[k] for k in chosen], width, w_gate_up[0], w_down[0])
        for k in reversed(chosen):
            sent = found[4 + k - low]
            returned[k] = flip(sent, "exp", k, groups) if k else sent
        parts.append(found)

    levels = blocks_total.bit_length() - 1
    rising = list(range(levels))
    turned = rising[1:] + rising[:1]
    hidden_units = w_down.shape[1]
    by_rows = (width // blocks_total) % LANES != 0
    lefts = [part[0].T if by_rows else part[0] for part in parts]
    grad_boths = [part[3] for part in parts]
    ups = [
        ScatterSum(lefts, grad_boths, at, hidden_units, "ctx", rising, by_rows, width)
        for at in range(2)
    ]
    down = ScatterSum(
        [part[1].T for part in parts], [part[2] for part in parts],
        0, width, "ctx", turned, True, hidden_units,
    )
    for one in (ups[0], down, ups[1]):
        one.step()

    def unpack(low):
        chosen = range(low, low + near)
        return contract_rows(
            jnp.concatenate([placing[k] for k in chosen], axis=0),
            jnp.concatenate([returned[k] for k in chosen], axis=0),
        )

    pair_grads = unpack(0) + unpack(near)
    grad_resid = (grad_out.astype(jnp.float32) + pair_grads[:, :width]).astype(jnp.bfloat16)
    grad_gates = pair_grads[:, width : width + 1].astype(jnp.bfloat16)

    pieces = {0: grad_resid}
    heads_width = w_out.shape[0]
    attn_grad = jnp.zeros((rows * groups, heads_width), jnp.bfloat16)
    for k in range(1, groups):
        low = k & -k
        pieces[k] = flip(pieces[k - low], "exp", low, groups)
    for k in range(groups):
        piece = contract_cols(pieces[k], w_out).astype(jnp.bfloat16)
        attn_grad = lax.dynamic_update_slice(attn_grad, piece, ((mine ^ k) * rows, 0))
        if k == 0:
            ups[0].step(attn_grad)
            down.step(attn_grad)
    ups[1].step(attn_grad)

    head_dim = prefix_state.shape[-1]
    tokens = attn_query.shape[0]
    heads = attn_query.shape[1] // head_dim
    block_at = lax.axis_index("ctx")
    counts = (
        3 * tokens * blocks_total + block_at * tokens + jnp.arange(tokens, dtype=jnp.int32) + 1
    ).astype(jnp.float32)
    inverse = jnp.broadcast_to((1.0 / counts)[:, None], (tokens, head_dim))

    per_head = pl.BlockSpec((tokens, head_dim), lambda h: (0, h))
    fixed = pl.BlockSpec((tokens, head_dim), lambda h: (0, 0))
    one_state = pl.BlockSpec((1, head_dim, head_dim), lambda h: (h, 0, 0))
    flat = jax.ShapeDtypeStruct((tokens, heads * head_dim), jnp.bfloat16)
    states = jax.ShapeDtypeStruct((heads, head_dim, head_dim), jnp.float32)
    chunk = min(256, tokens)

    size = 2 * tokens * heads * head_dim
    local_state, grad_scaled = pl.pallas_call(
        state_kernel,
        grid=(heads,),
        in_specs=[per_head, per_head, fixed],
        out_specs=[one_state, per_head],
        out_shape=[states, flat],
        cost_estimate=cost(size * head_dim, 3 * size),
        name="state",
    )(attn_query, attn_grad, inverse)

    later = jnp.zeros_like(local_state)
    step = 1
    results = {}
    while step < blocks_total:
        held = (local_state + later).astype(jnp.bfloat16)
        came = lax.ppermute(held, "ctx", [(i, i - step) for i in range(step, blocks_total)])
        for name, one in (("up0", ups[0]), ("down", down), ("up1", ups[1])):
            if name not in results and (name != "up1" or step > 1):
                got = one.step(held)
                if got is not None:
                    results[name] = got
        later = later + came.astype(jnp.float32)
        step *= 2

    grad_query = pl.pallas_call(
        functools.partial(forward_kernel, chunk),
        grid=(heads,),
        in_specs=[per_head, per_head, per_head, fixed, one_state],
        out_specs=per_head,
        out_shape=flat,
        cost_estimate=cost(size * (2 * chunk + 2 * head_dim), 4 * size),
        name="forward",
    )(attn_key, attn_value, attn_grad, inverse, prefix_state[0])
    grad_key, grad_value = pl.pallas_call(
        functools.partial(backward_kernel, chunk),
        grid=(heads,),
        in_specs=[per_head, per_head, per_head, per_head, one_state],
        out_specs=[per_head, per_head],
        out_shape=[flat, flat],
        cost_estimate=cost(size * (4 * chunk + 3 * head_dim), 6 * size),
        name="backward",
    )(attn_query, attn_key, attn_value, grad_scaled, later)
    for name, one in (("up0", ups[0]), ("down", down), ("up1", ups[1])):
        while name not in results:
            got = one.step()
            if got is not None:
                results[name] = got
    grad_gate_up = jnp.concatenate([results["up0"], results["up1"]], axis=2)
    grad_down = results["down"]
    return grad_query, grad_key, grad_value, grad_resid, grad_gates, grad_gate_up, grad_down


def solution(mesh):
    return jax.shard_map(
        compute,
        mesh=mesh,
        in_specs=(
            P("ctx", "exp"),
            P("ctx", "exp"),
            P("ctx", "exp"),
            P("ctx", "exp", None, None),
            P(("ctx", "exp"), None),
            P(("ctx", "exp"), None),
            P(("ctx", "exp"), None),
            P(("ctx", "exp"), None),
            P("exp", None, None),
            P("exp", None, None),
            P("exp", None),
        ),
        out_specs=(
            P("ctx", "exp"),
            P("ctx", "exp"),
            P("ctx", "exp"),
            P(("ctx", "exp"), None),
            P(("ctx", "exp"), None),
            P("exp", "ctx", None),
            P("exp", "ctx", None),
        ),
        check_vma=False,
    )
```

```python
import functools

import jax
import jax.numpy as jnp
from jax import lax
from jax.experimental import pallas as pl
from jax.experimental.pallas import tpu as pltpu
from jax.sharding import PartitionSpec as P

LANES = 128


def contract_rows(left, right):
    return lax.dot_general(
        left, right, (((0,), (0,)), ((), ())), preferred_element_type=jnp.float32
    )


def contract_cols(left, right):
    return lax.dot_general(
        left, right, (((1,), (1,)), ((), ())), preferred_element_type=jnp.float32
    )


def plain(left, right):
    return jnp.dot(left, right, preferred_element_type=jnp.float32)


def flip(value, axis, bit, size):
    return lax.ppermute(value, axis, [(i, i ^ bit) for i in range(size)])


def expert_kernel(near, width, *refs):
    blocks, (pair_ref, back_ref) = refs[:near], refs[near : near + 2]
    rows_ref, hidden_ref, scaled_ref, both_ref = refs[near + 2 : near + 6]
    outs = refs[near + 6 :]
    capacity = blocks[0].shape[0]
    hidden_units = back_ref.shape[0]
    for at, block in enumerate(blocks):
        rows_ref[pl.ds(at * capacity, capacity), :] = block[:, :width]
    cot_wide = jnp.concatenate([block[:, width : 2 * width] for block in blocks], axis=0).astype(
        jnp.float32
    )
    gate_vals = jnp.concatenate([block[:, 2 * width :] for block in blocks], axis=0)
    scaled = (gate_vals[:, :1].astype(jnp.float32) * cot_wide).astype(jnp.bfloat16)
    scaled_ref[...] = scaled
    both = plain(rows_ref[...], pair_ref[...])
    first = both[:, :hidden_units]
    second = both[:, hidden_units:]
    logistic = jax.nn.sigmoid(first)
    silu = first * logistic
    hidden = (silu * second).astype(jnp.bfloat16)
    hidden_ref[...] = hidden
    grad_hidden = contract_cols(scaled, back_ref[...])
    slope = logistic * (1.0 + first * (1.0 - logistic))
    both_ref[:, :hidden_units] = (grad_hidden * second * slope).astype(jnp.bfloat16)
    both_ref[:, hidden_units:] = (grad_hidden * silu).astype(jnp.bfloat16)
    output = plain(hidden, back_ref[...])
    grad_gate = jnp.sum(cot_wide * output, axis=1, keepdims=True)
    grad_rows = contract_cols(both_ref[...], pair_ref[...]).astype(jnp.bfloat16)
    for at, out in enumerate(outs):
        rows = slice(at * capacity, (at + 1) * capacity)
        out[:, :width] = grad_rows[rows]
        out[:, width:] = jnp.broadcast_to(grad_gate[rows], (capacity, LANES)).astype(jnp.bfloat16)


def expert_backward(blocks, width, w_pair, w_back):
    near = len(blocks)
    capacity = blocks[0].shape[0]
    tokens = near * capacity
    hidden_units = w_back.shape[0]

    def shape(*dims):
        return jax.ShapeDtypeStruct(dims, jnp.bfloat16)

    outs = [shape(tokens, width), shape(tokens, hidden_units), shape(tokens, width)]
    outs += [shape(tokens, 2 * hidden_units)] + [shape(capacity, width + LANES)] * near
    whole = pl.BlockSpec(memory_space=pltpu.VMEM)
    return pl.pallas_call(
        functools.partial(expert_kernel, near, width),
        in_specs=[whole] * (near + 2),
        out_specs=[whole] * len(outs),
        out_shape=outs,
        cost_estimate=cost(12 * tokens * width * hidden_units, 24 * hidden_units * width),
        name="expert",
    )(*blocks, w_pair, w_back)


def after(value, *others):
    return lax.optimization_barrier((value,) + others)[0]


def cost(flops, moved):
    return pl.CostEstimate(flops=flops, bytes_accessed=moved, transcendentals=0)


def partial_kernel(by_rows, parts, me_ref, *refs):
    lefts, rights, came, out_ref = refs[:parts], refs[parts : 2 * parts], refs[2 * parts : -1], refs[-1]
    multiply = plain if by_rows else contract_rows
    total = multiply(lefts[0][...], rights[0][...])
    for left_ref, right_ref in zip(lefts[1:], rights[1:]):
        total = total + multiply(left_ref[...], right_ref[...])
    for one in came:
        total = total + one[0].astype(jnp.float32)
    out_ref[0] = total.astype(out_ref.dtype)


class ScatterSum:
    def __init__(self, lefts, rights, at, cols, axis, bits, by_rows, rows):
        self.lefts, self.rights, self.at, self.cols = lefts, rights, at, cols
        self.axis, self.bits, self.by_rows = axis, bits, by_rows
        self.size = lax.axis_size(axis)
        self.unit = rows // self.size
        self.me = lax.axis_index(axis).astype(jnp.int32).reshape(1)
        self.came = []

    def step(self, *ties):
        bits, stage, unit, cols, at = self.bits, len(self.came), self.unit, self.cols, self.at
        last = stage == len(bits)
        free = sorted(set(bits) - set(bits[: stage + 1]))

        def chunk(j, me_ref):
            own = me_ref[0]
            found = 0
            for bit in bits[: stage + 1]:
                found = found | (own & (1 << bit))
            if not last:
                found = found ^ (1 << bits[stage])
            for place, bit in enumerate(free):
                found = found | (((j >> place) & 1) << bit)
            return found

        def spot(upto):
            kept = sorted(set(bits) - set(bits[:upto]))

            def index(j, me_ref):
                found = chunk(j, me_ref)
                where = 0 * j
                for place, bit in enumerate(kept):
                    where = where | (((found >> bit) & 1) << place)
                return (where, 0, 0)

            return index

        steps = 1 << len(free)
        depth = self.rights[0].shape[0]
        if self.by_rows:
            left_spec = pl.BlockSpec((unit, depth), lambda j, me_ref: (chunk(j, me_ref), 0))
        else:
            left_spec = pl.BlockSpec((depth, unit), lambda j, me_ref: (0, chunk(j, me_ref)))
        right_spec = pl.BlockSpec((depth, cols), lambda j, me_ref: (0, at))
        parts = len(self.lefts)
        came = self.came
        if ties and came:
            came = came[:-1] + [after(came[-1], *ties)]
        kind = jnp.float32 if last else jnp.bfloat16
        out = pl.pallas_call(
            functools.partial(partial_kernel, self.by_rows, parts),
            grid_spec=pltpu.PrefetchScalarGridSpec(
                num_scalar_prefetch=1,
                grid=(steps,),
                in_specs=[left_spec] * parts
                + [right_spec] * parts
                + [pl.BlockSpec((1, unit, cols), spot(i + 1)) for i in range(stage)],
                out_specs=pl.BlockSpec((1, unit, cols), lambda j, me_ref: (j, 0, 0)),
            ),
            out_shape=jax.ShapeDtypeStruct((steps, unit, cols), kind),
            cost_estimate=cost(2 * parts * depth * unit * cols * steps, 4 * steps * unit * cols + 2 * depth * cols),
        )(self.me, *self.lefts, *self.rights, *came)
        if last:
            return out
        self.came = came + [flip(out, self.axis, 1 << bits[stage], self.size)]
        return None


def inverse_counts(place_ref, start, shape):
    counts = place_ref[1] + start + 1 + lax.broadcasted_iota(jnp.int32, shape, 0)
    return 1.0 / counts.astype(jnp.float32)


def project_kernel(groups, place_ref, *refs):
    pieces, (w_ref, query_ref), (grad_ref, scaled_ref, state_ref, sent_ref) = (
        refs[:groups],
        refs[groups : groups + 2],
        refs[groups + 2 :],
    )
    rows = pieces[0].shape[0]
    heads, head_dim = state_ref.shape[:2]
    width = heads * head_dim
    for k in range(groups):
        start = pl.multiple_of((place_ref[0] ^ k) * rows, rows)
        at = pl.ds(start, rows)
        grads = contract_cols(pieces[k][...], w_ref[...]).astype(jnp.bfloat16)
        inverse = inverse_counts(place_ref, start, (rows, width))
        scaled = (grads.astype(jnp.float32) * inverse).astype(jnp.bfloat16)
        grad_ref[at, :] = grads
        scaled_ref[at, :] = scaled
        for h in range(heads):
            cols = slice(h * head_dim, (h + 1) * head_dim)
            state = contract_rows(query_ref[at, cols], scaled[:, cols])
            if k:
                state = state + state_ref[h]
            state_ref[h] = state
            if k == groups - 1:
                sent_ref[h] = state.astype(jnp.bfloat16)


def forward_kernel(chunk, place_ref, key_ref, value_ref, grad_ref, prior_ref, out_ref):
    tokens = key_ref.shape[0]
    row = lax.broadcasted_iota(jnp.int32, (chunk, chunk), 0)
    col = lax.broadcasted_iota(jnp.int32, (chunk, chunk), 1)
    state = prior_ref[0]
    for at in range(tokens // chunk):
        rows = pl.ds(at * chunk, chunk)
        keys, values, grads = key_ref[rows, :], value_ref[rows, :], grad_ref[rows, :]
        mix = jnp.where(col <= row, contract_cols(grads, values), 0.0).astype(jnp.bfloat16)
        out = plain(mix, keys) + contract_cols(grads, state.astype(jnp.bfloat16))
        out_ref[rows, :] = (out * inverse_counts(place_ref, at * chunk, out.shape)).astype(jnp.bfloat16)
        state = state + contract_rows(keys, values)


def backward_kernel(chunk, query_ref, key_ref, value_ref, scaled_ref, later_ref, dkey_ref, dvalue_ref):
    tokens = key_ref.shape[0]
    row = lax.broadcasted_iota(jnp.int32, (chunk, chunk), 0)
    col = lax.broadcasted_iota(jnp.int32, (chunk, chunk), 1)
    state = later_ref[0]
    for at in reversed(range(tokens // chunk)):
        rows = pl.ds(at * chunk, chunk)
        query, keys, values, scaled = query_ref[rows, :], key_ref[rows, :], value_ref[rows, :], scaled_ref[rows, :]
        held = state.astype(jnp.bfloat16)
        mix_key = jnp.where(col >= row, contract_cols(values, scaled), 0.0).astype(jnp.bfloat16)
        dkey_ref[rows, :] = (plain(mix_key, query) + contract_cols(values, held)).astype(jnp.bfloat16)
        mix_value = jnp.where(col >= row, contract_cols(keys, query), 0.0).astype(jnp.bfloat16)
        dvalue_ref[rows, :] = (plain(mix_value, scaled) + plain(keys, held)).astype(jnp.bfloat16)
        state = state + contract_rows(query, scaled)


def compute(
    attn_query,
    attn_key,
    attn_value,
    prefix_state,
    moe_in,
    grad_out,
    router_gates,
    expert_ids,
    w_gate_up,
    w_down,
    w_out,
):
    groups = lax.axis_size("exp")
    blocks_total = lax.axis_size("ctx")
    flight = w_gate_up.shape[0] * groups
    rows, width = moe_in.shape
    capacity = 3 * rows // (2 * flight)
    flat_ids = expert_ids.reshape(rows)
    place = jnp.arange(rows, dtype=jnp.int32)
    same = (flat_ids[:, None] == flat_ids[None, :]) & (place[:, None] < place[None, :])
    slot_of = jnp.sum(same.astype(jnp.int32), axis=0)
    mine = lax.axis_index("exp")
    target = (flat_ids ^ mine) * capacity + slot_of
    joined = jnp.concatenate(
        [moe_in, grad_out, jnp.broadcast_to(router_gates, (rows, LANES))], axis=1
    )
    place = jnp.arange(capacity, dtype=jnp.int32)[:, None]
    placing = {
        k: (place + k * capacity == target[None, :]).astype(jnp.bfloat16) for k in range(groups)
    }
    arrived = {}
    for k in reversed(range(groups)):
        packed = plain(placing[k], joined).astype(jnp.bfloat16)
        arrived[k] = flip(packed, "exp", k, groups) if k else packed
    near = groups // 2
    parts, returned = [], {}
    for low in (0, near):
        chosen = range(low, low + near)
        found = expert_backward([arrived[k] for k in chosen], width, w_gate_up[0], w_down[0])
        for k in reversed(chosen):
            sent = found[4 + k - low]
            returned[k] = flip(sent, "exp", k, groups) if k else sent
        parts.append(found)

    levels = blocks_total.bit_length() - 1
    rising = list(range(levels))
    turned = rising[1:] + rising[:1]
    hidden_units = w_down.shape[1]
    by_rows = (width // blocks_total) % LANES != 0
    lefts = [part[0].T if by_rows else part[0] for part in parts]
    grad_boths = [part[3] for part in parts]
    up = ScatterSum(
        lefts, grad_boths, 0, 2 * hidden_units, "ctx", rising, by_rows, width
    )
    down = ScatterSum(
        [part[1].T for part in parts], [part[2] for part in parts],
        0, width, "ctx", turned, True, hidden_units,
    )
    for one in (up, down):
        one.step()

    def unpack(low):
        chosen = range(low, low + near)
        return contract_rows(
            jnp.concatenate([placing[k] for k in chosen], axis=0),
            jnp.concatenate([returned[k] for k in chosen], axis=0),
        )

    pair_grads = unpack(0) + unpack(near)
    grad_resid = (grad_out.astype(jnp.float32) + pair_grads[:, :width]).astype(jnp.bfloat16)
    grad_gates = pair_grads[:, width : width + 1].astype(jnp.bfloat16)

    pieces = {0: grad_resid}
    for k in range(1, groups):
        low = k & -k
        pieces[k] = flip(pieces[k - low], "exp", low, groups)
    down.step(grad_resid)

    head_dim = prefix_state.shape[-1]
    tokens = attn_query.shape[0]
    heads = attn_query.shape[1] // head_dim
    block_at = lax.axis_index("ctx")
    place = jnp.stack([mine, (3 * blocks_total + block_at) * tokens]).astype(jnp.int32)

    per_head = pl.BlockSpec((tokens, head_dim), lambda h: (0, h))
    scalars = pl.BlockSpec(memory_space=pltpu.SMEM)
    whole = pl.BlockSpec(memory_space=pltpu.VMEM)
    one_state = pl.BlockSpec((1, head_dim, head_dim), lambda h: (h, 0, 0))
    flat = jax.ShapeDtypeStruct((tokens, heads * head_dim), jnp.bfloat16)
    states = jax.ShapeDtypeStruct((heads, head_dim, head_dim), jnp.float32)
    chunk = min(256, tokens)

    size = 2 * tokens * heads * head_dim
    attn_grad, grad_scaled, local_state, held = pl.pallas_call(
        functools.partial(project_kernel, groups),
        in_specs=[scalars] + [whole] * (groups + 2),
        out_specs=[whole] * 4,
        out_shape=[flat, flat, states, jax.ShapeDtypeStruct(states.shape, jnp.bfloat16)],
        cost_estimate=cost(size * (width + head_dim), 4 * size + 2 * tokens * width),
        name="project",
    )(place, *[pieces[k] for k in range(groups)], w_out, attn_query)

    later = jnp.zeros_like(local_state)
    step = 1
    results = {}
    while step < blocks_total:
        came = lax.ppermute(held, "ctx", [(i, i - step) for i in range(step, blocks_total)])
        if step == 1:
            up.step(held)
        elif step == 2:
            results["down"] = down.step(held)
        later = later + came.astype(jnp.float32)
        held = (local_state + later).astype(jnp.bfloat16)
        step *= 2

    grad_query = pl.pallas_call(
        functools.partial(forward_kernel, chunk),
        grid=(heads,),
        in_specs=[scalars, per_head, per_head, per_head, one_state],
        out_specs=per_head,
        out_shape=flat,
        cost_estimate=cost(size * (2 * chunk + 2 * head_dim), 4 * size),
        name="forward",
    )(place, attn_key, attn_value, attn_grad, prefix_state[0])
    grad_key, grad_value = pl.pallas_call(
        functools.partial(backward_kernel, chunk),
        grid=(heads,),
        in_specs=[per_head, per_head, per_head, per_head, one_state],
        out_specs=[per_head, per_head],
        out_shape=[flat, flat],
        cost_estimate=cost(size * (4 * chunk + 3 * head_dim), 6 * size),
        name="backward",
    )(attn_query, attn_key, attn_value, grad_scaled, later)
    for name, one in (("up", up), ("down", down)):
        while results.get(name) is None:
            results[name] = one.step()
    grad_gate_up, grad_down = results["up"], results["down"]
    return grad_query, grad_key, grad_value, grad_resid, grad_gates, grad_gate_up, grad_down


def solution(mesh):
    return jax.shard_map(
        compute,
        mesh=mesh,
        in_specs=(
            P("ctx", "exp"),
            P("ctx", "exp"),
            P("ctx", "exp"),
            P("ctx", "exp", None, None),
            P(("ctx", "exp"), None),
            P(("ctx", "exp"), None),
            P(("ctx", "exp"), None),
            P(("ctx", "exp"), None),
            P("exp", None, None),
            P("exp", None, None),
            P("exp", None),
        ),
        out_specs=(
            P("ctx", "exp"),
            P("ctx", "exp"),
            P("ctx", "exp"),
            P(("ctx", "exp"), None),
            P(("ctx", "exp"), None),
            P("exp", "ctx", None),
            P("exp", "ctx", None),
        ),
        check_vma=False,
    )
```
